128 devices in a mesh: group: 4 (over y_hi, core), member: 32 (over x, y_lo, z).
Axes of the slice: x: 4, y: 4 (y_hi: 2, y_lo: 2; y = y_hi * 2 + y_lo), z: 4, core: 2. Of those that a mesh axis runs over, the one named last changes fastest.
Arguments:
- face_schur: float32 [512, 6, 256, 256], P(('group', 'member')), as said below
- face_inverse: float32 [512, 6, 256, 256], P(('group', 'member')), as said below
- face_basis: float32 [512, 6, 96, 256], P(('group', 'member')), may hold values from -6 to 6
- partner: int32 [512, 6], P(('group', 'member')), may hold values from 0 to 3071, as said below
- prim_index: int32 [512, 96], P(('group', 'member')), may hold values from 0 to 24575
Outputs:
- deluxe_basis: float32 [512, 6, 96, 256], P(('group', 'member'))
- coarse_blocks: float32 [512, 9216], P('group')
The draws below stay inside these ranges and needn't reach their ends.
Inputs may be any that keep to these rules, and one draw needn't show every extreme that they name: partner pairs the faces: the partner of the partner of a face is the face itself; a face of subdomain s has its partner on another device of the same group, where subdomain s lies on device s // 4 and devices k * 32 to (k + 1) * 32 - 1 form group k; at most 1 faces of one device have partners on one other device, and some pair of devices has exactly 1. Every block of face_schur is exactly symmetric and positive definite. Every block of face_inverse is exactly symmetric.
All inputs are finite; a program needn't handle non-finite values.
Results may differ from the reference program's by a relative error of at most 0.0003.
Values sent between devices are 32-bit elements; how exact they have to be, the bound alone decides.
No kernel may reach another device: no remote copies, remote signals or barrier semaphores. Data moves between devices by JAX's collectives and lax.ppermute only.
A program may use at most 128 MiB of HBM per device.

```python
import jax
import jax.numpy as jnp
from jax import lax

FACE = 256
NPRIM = 96
SWEEPS = 2
GROUPS = 4
MEMBERS = 32
SUBDOMAINS = 512
FACES_DEV = 24
PEER_CAP = 1
COARSE_COUNT = 24576


def face_pair(key):
    scale_key = jax.random.fold_in(key, 101)
    noise_key = jax.random.fold_in(key, 202)
    extra_key = jax.random.fold_in(key, 303)
    jitter_key = jax.random.fold_in(key, 404)
    diagonal_values = jnp.exp(jax.random.uniform(scale_key, (SUBDOMAINS, 6, FACE), jnp.float32, 0.0, 0.6931472))
    noise = jnp.clip(jax.random.normal(noise_key, (SUBDOMAINS, 6, FACE, FACE), jnp.float32), -4.0, 4.0)
    identity = jnp.eye(FACE, dtype=jnp.float32)
    coupling = 0.0141421 * (noise + jnp.swapaxes(noise, -1, -2)) * (1.0 - identity)
    schur_block = identity * diagonal_values[..., None] + coupling
    extra_noise = jnp.clip(jax.random.normal(extra_key, (SUBDOMAINS, 6, FACE, FACE), jnp.float32), -4.0, 4.0)
    roots = jnp.sqrt(diagonal_values)
    perturbation = 0.0133 * (extra_noise + jnp.swapaxes(extra_noise, -1, -2)) * (1.0 - identity) / (roots[..., :, None] * roots[..., None, :])
    jitter = jax.random.uniform(jitter_key, (SUBDOMAINS, 6, FACE), jnp.float32, -1.0, 1.0)
    inverse_diagonal = (1.0 + 0.1 * jitter) / diagonal_values
    inverse_block = identity * inverse_diagonal[..., None] - coupling / (diagonal_values[..., :, None] * diagonal_values[..., None, :]) + perturbation
    return (schur_block, inverse_block)


def draw_face_schur(key, part):
    return face_pair(key)[0]


def draw_face_inverse(key, part):
    return face_pair(key)[1]


def draw_partner(key, part):
    member_count = MEMBERS
    face_count = FACES_DEV
    group_keys = jax.random.split(key, GROUPS)

    def one_group(group_key, group_number):
        label_key = jax.random.fold_in(group_key, 1)
        order_key = jax.random.fold_in(group_key, 2)
        slot_key = jax.random.fold_in(group_key, 3)
        labels = jax.random.permutation(label_key, member_count).astype(jnp.int32)
        xor_values = (jax.random.permutation(order_key, member_count - 1) + 1).astype(jnp.int32)
        slot_xor = jnp.tile(xor_values, PEER_CAP)[:face_count]
        placements = jax.vmap(lambda single_key: jax.random.permutation(single_key, face_count))(jax.random.split(slot_key, member_count)).astype(jnp.int32)
        virtual = jnp.arange(member_count, dtype=jnp.int32)[:, None]
        partner_virtual = jnp.bitwise_xor(virtual, slot_xor[None, :])
        slot_column = jnp.broadcast_to(jnp.arange(face_count, dtype=jnp.int32)[None, :], (member_count, face_count))
        partner_local = placements[partner_virtual, slot_column]
        partner_global = (group_number * member_count + labels[partner_virtual]) * face_count + partner_local
        row_labels = jnp.broadcast_to(labels[:, None], (member_count, face_count))
        result = jnp.zeros((member_count, face_count), jnp.int32)
        return result.at[row_labels, placements].set(partner_global.astype(jnp.int32))
    grouped = jax.vmap(one_group)(group_keys, jnp.arange(GROUPS, dtype=jnp.int32))
    return grouped.reshape(SUBDOMAINS, 6).astype(jnp.int32)


def touch_ends(entries, rng, low, largest):
    longest = entries.shape.index(max(entries.shape))
    spots = []
    for shift in (0, 1):
        where = [jax.random.randint(jax.random.fold_in(rng, axis), (), 0, length) for axis, length in enumerate(entries.shape)]
        where[longest] = (where[longest] + shift) % entries.shape[longest]
        spots.append(tuple(where))
    return entries.at[spots[0]].set(low).at[spots[1]].set(largest)


def shard_levels(stream_key, dims, pieces, smallest, top_value):
    level = 1.0
    for axis_at, parts in pieces:
        steps = jax.random.uniform(jax.random.fold_in(jax.random.fold_in(stream_key, 6), axis_at), (parts,), jnp.float32, smallest / len(pieces), top_value / len(pieces))
        level = level * jnp.repeat(jnp.exp(steps), dims[axis_at] // parts).reshape((-1,) + (1,) * (len(dims) - 1 - axis_at))
    return level


def scatter_about(key, dims, scale, limit, cuts=(), kind=jnp.bfloat16):
    loudness = shard_levels(key, dims, cuts, -0.22, 0.18) if cuts else 1.0
    entries = jax.random.normal(key, dims, jnp.float32) * scale * loudness
    return jnp.minimum(jnp.maximum(entries, -limit), limit).astype(kind)


def setup_inputs(seed: int = 0) -> dict:
    splits = jax.random.split(jax.random.key(seed), 6)
    return {
        "face_schur": draw_face_schur(jax.random.fold_in(splits[5], 71), 0),
        "face_inverse": draw_face_inverse(jax.random.fold_in(splits[5], 71), 0),
        "face_basis": scatter_about(splits[2], (SUBDOMAINS, 6, NPRIM, FACE), 1.0, 6.0, ((0, 128),), jnp.float32),
        "partner": draw_partner(jax.random.fold_in(splits[5], 71), 0),
        "prim_index": touch_ends(jax.random.randint(splits[4], (SUBDOMAINS, NPRIM), 0, COARSE_COUNT), jax.random.fold_in(splits[4], 1), 0, COARSE_COUNT - 1).astype(jnp.int32),
    }


FULL_PRECISION = lax.Precision.HIGHEST

def inverse_sweeps(summed, initial):
    doubled = 2.0 * jnp.eye(summed.shape[-1], dtype=jnp.float32)
    current = initial
    for repeat in range(SWEEPS):
        applied = jnp.einsum('fij,fjk->fik', summed, current, precision=FULL_PRECISION)
        current = jnp.einsum('fij,fjk->fik', current, doubled - applied, precision=FULL_PRECISION)
    return current

def face_terms(own_schur, other_schur, own_inverse, other_inverse, basis):
    summed = own_schur + other_schur
    approx_inverse = inverse_sweeps(summed, 0.25 * (own_inverse + other_inverse))
    product = jnp.einsum('fck,fjk->fcj', basis, own_schur, precision=FULL_PRECISION)
    deluxe = jnp.einsum('fck,fik->fci', product, approx_inverse, precision=FULL_PRECISION)
    weighted = jnp.einsum('fci,fij->fcj', deluxe, other_schur, precision=FULL_PRECISION)
    face_block = jnp.einsum('fcj,fdj->fcd', weighted, deluxe, precision=FULL_PRECISION)
    return (deluxe, face_block)

def reference(face_schur, face_inverse, face_basis, partner, prim_index):
    subdomain_count = face_schur.shape[0]
    face_width = face_schur.shape[-1]
    flat_schur = face_schur.reshape(subdomain_count * 6, face_width, face_width)
    flat_inverse = face_inverse.reshape(subdomain_count * 6, face_width, face_width)

    def one_subdomain(position):
        targets = partner[position].astype(jnp.int32)
        other_schur = jnp.take(flat_schur, targets, axis=0)
        other_inverse = jnp.take(flat_inverse, targets, axis=0)
        deluxe, face_block = face_terms(face_schur[position], other_schur, face_inverse[position], other_inverse, face_basis[position])
        return (deluxe, lax.optimization_barrier(jnp.sum(face_block, axis=0)))
    deluxe_basis, galerkin = lax.map(one_subdomain, jnp.arange(subdomain_count, dtype=jnp.int32))
    diagonal_terms = jnp.diagonal(galerkin, axis1=1, axis2=2)
    coarse_diagonal = jnp.zeros((COARSE_COUNT,), jnp.float32).at[prim_index.reshape(-1)].add(diagonal_terms.reshape(-1))
    scales = 1.0 / jnp.sqrt(coarse_diagonal[prim_index])
    scaled = scales[:, :, None] * galerkin * scales[:, None, :]
    coarse_blocks = scaled.reshape(subdomain_count, galerkin.shape[1] * galerkin.shape[2])
    return (deluxe_basis, coarse_blocks)
```

```python
import jax
import jax.numpy as jnp
from jax import lax
from jax.experimental import pallas as pl
from jax.experimental.pallas import tpu as pltpu
from jax.sharding import PartitionSpec as P

AXES = ("group", "member")
COARSE_PER_SUB = 48
LANES = 128


def iotas(rows, cols):
    return (
        lax.broadcasted_iota(jnp.int32, (rows, cols), 0),
        lax.broadcasted_iota(jnp.int32, (rows, cols), 1),
    )


def halves(value):
    high = value.astype(jnp.bfloat16)
    return high, (value - high.astype(jnp.float32)).astype(jnp.bfloat16)


def dot(left, right, right_dim=0):
    dims = (((1,), (right_dim,)), ((), ()))
    rows = left[0].shape[0]
    stacked = jnp.concatenate(left, axis=0)
    first = lax.dot_general(stacked, right[0], dims, preferred_element_type=jnp.float32)
    second = lax.dot_general(left[0], right[1], dims, preferred_element_type=jnp.float32)
    return first[:rows] + (first[rows:] + second)


def pack_kernel(slot_ref, schur_ref, inverse_ref, out_ref):
    width = schur_ref.shape[1]
    schur, inverse = schur_ref[0], inverse_ref[0]
    row, col = iotas(width, width)
    packed = jnp.where(row <= col, schur, inverse)
    diagonal = jnp.sum(jnp.where(row == col, inverse, 0.0), axis=0, keepdims=True)
    parts = width // LANES
    for part in range(parts):
        lanes = slice(part * LANES, (part + 1) * LANES)
        out_ref[0, part * width : (part + 1) * width, :] = packed[:, lanes]
        out_ref[0, parts * width + part : parts * width + part + 1, :] = diagonal[:, lanes]


def pack(slots, schur, inverse, members):
    faces, width = schur.shape[:2]
    rows = width * width // LANES + 8
    block = pl.BlockSpec((1, width, width), lambda f, slot: (f, 0, 0))
    return pl.pallas_call(
        pack_kernel,
        out_shape=jax.ShapeDtypeStruct((members, rows, LANES), jnp.float32),
        grid_spec=pltpu.PrefetchScalarGridSpec(
            num_scalar_prefetch=1,
            grid=(faces,),
            in_specs=[block, block],
            out_specs=pl.BlockSpec((1, rows, LANES), lambda f, slot: (slot[f], 0, 0)),
        ),
        name="pack_faces",
    )(slots, schur, inverse)


def face_kernel(slot_ref, schur_ref, inverse_ref, basis_ref, *rest):
    per_step = schur_ref.shape[0]
    received = rest[:per_step]
    deluxe_ref, galerkin_ref, diagonal_ref = rest[per_step:]
    width = schur_ref.shape[1]
    prims = basis_ref.shape[1]
    parts = width // LANES
    steps_per_sub = 6 // per_step
    step = pl.program_id(0)
    row, col = iotas(width, width)
    total = None
    for face in range(per_step):
        mixed = jnp.concatenate(
            [received[face][0, p * width : (p + 1) * width, :] for p in range(parts)], axis=1
        )
        line = jnp.concatenate(
            [received[face][0, parts * width + p : parts * width + p + 1, :] for p in range(parts)], axis=1
        )
        turned = mixed.T
        other_schur = jnp.where(row <= col, mixed, turned)
        other_inverse = jnp.where(row > col, mixed, jnp.where(row == col, line, turned))
        schur = schur_ref[face]
        summed = halves(schur + other_schur)
        initial = halves(0.25 * (inverse_ref[face] + other_inverse))
        residual = halves(jnp.where(row == col, 1.0, 0.0) - dot(summed, initial))
        product = dot(halves(basis_ref[face]), halves(schur))
        start = dot(halves(product), initial)
        deluxe = start
        for _ in range(3):
            deluxe = start + dot(halves(deluxe), residual)
        deluxe_ref[face] = deluxe
        deluxe = halves(deluxe)
        weighted = dot(deluxe, halves(other_schur))
        block = dot(halves(weighted), deluxe, right_dim=1)
        total = block if total is None else total + block

    @pl.when(step == 0)
    def _():
        diagonal_ref[...] = jnp.zeros_like(diagonal_ref)

    @pl.when(step % steps_per_sub == 0)
    def _():
        galerkin_ref[0] = total

    @pl.when(step % steps_per_sub != 0)
    def _():
        galerkin_ref[0] += total

    @pl.when(step % steps_per_sub == steps_per_sub - 1)
    def _():
        row, col = iotas(prims, prims)
        line = jnp.sum(jnp.where(row == col, galerkin_ref[0], 0.0), axis=0, keepdims=True)
        diagonal_ref[pl.ds(step // steps_per_sub, 1), 0:prims] = line


def faces(slots, schur, inverse, basis, received, subs):
    count, width = schur.shape[:2]
    prims = basis.shape[1]
    rows = received.shape[1]
    per_step = 2
    steps_per_sub = 6 // per_step
    block = pl.BlockSpec((per_step, width, width), lambda i, slot: (i, 0, 0))
    thin = pl.BlockSpec((per_step, prims, width), lambda i, slot: (i, 0, 0))

    def incoming(offset):
        return pl.BlockSpec((1, rows, LANES), lambda i, slot: (slot[i * per_step + offset], 0, 0))

    return pl.pallas_call(
        face_kernel,
        out_shape=(
            jax.ShapeDtypeStruct((count, prims, width), jnp.float32),
            jax.ShapeDtypeStruct((subs, prims, prims), jnp.float32),
            jax.ShapeDtypeStruct((8, LANES), jnp.float32),
        ),
        grid_spec=pltpu.PrefetchScalarGridSpec(
            num_scalar_prefetch=1,
            grid=(count // per_step,),
            in_specs=[block, block, thin] + [incoming(o) for o in range(per_step)],
            out_specs=(
                thin,
                pl.BlockSpec((1, prims, prims), lambda i, slot: (i // steps_per_sub, 0, 0)),
                pl.BlockSpec((8, LANES), lambda i, slot: (0, 0)),
            ),
        ),
        name="face_terms",
    )(slots, schur, inverse, basis, *([received] * per_step))


def table_kernel(index_ref, value_ref, table_ref):
    highs = table_ref.shape[0]
    rows = index_ref.shape[0]
    step = pl.program_id(0)
    high_iota = lax.broadcasted_iota(jnp.int32, (highs, LANES), 0)
    low_iota = lax.broadcasted_iota(jnp.int32, (LANES, LANES), 0)
    dims = (((1,), (1,)), ((), ()))
    left, right = [], ([], [])
    for r in range(rows):
        index = index_ref[r : r + 1, :]
        high, low = halves(value_ref[r : r + 1, :])
        left.append(jnp.where(high_iota == index // LANES, 1.0, 0.0).astype(jnp.bfloat16))
        hit = low_iota == index % LANES
        for part, value in enumerate((high, low)):
            wide = value.astype(jnp.float32)
            right[part].append(jnp.where(hit, wide, 0.0).astype(jnp.bfloat16))
    left = jnp.concatenate(left, axis=1)
    total = sum(
        lax.dot_general(left, jnp.concatenate(part, axis=1), dims, preferred_element_type=jnp.float32)
        for part in right
    )

    @pl.when(step == 0)
    def _():
        table_ref[...] = total

    @pl.when(step != 0)
    def _():
        table_ref[...] += total


def coarse_table(indices, values, coarse):
    rows = indices.shape[0]
    per_step = 16
    block = pl.BlockSpec((per_step, LANES), lambda i: (i, 0))
    return pl.pallas_call(
        table_kernel,
        out_shape=jax.ShapeDtypeStruct((coarse // LANES, LANES), jnp.float32),
        grid=(rows // per_step,),
        in_specs=[block, block],
        out_specs=pl.BlockSpec((coarse // LANES, LANES), lambda i: (0, 0)),
        name="coarse_table",
    )(indices, values)


def scale_kernel(index_ref, table_ref, galerkin_ref, out_ref):
    subs = index_ref.shape[0]
    prims = 96
    highs = table_ref.shape[0]
    table = halves(table_ref[...])
    high_iota = lax.broadcasted_iota(jnp.int32, (highs, LANES), 0)
    low_iota = lax.broadcasted_iota(jnp.int32, (LANES, LANES), 0)
    dims = (((0,), (0,)), ((), ()))
    scales = []
    for s in range(subs):
        index = index_ref[s : s + 1, :]
        hit = jnp.where(high_iota == index // LANES, 1.0, 0.0).astype(jnp.bfloat16)
        rows = sum(lax.dot_general(part, hit, dims, preferred_element_type=jnp.float32) for part in table)
        value = jnp.sum(jnp.where(low_iota == index % LANES, rows, 0.0), axis=0, keepdims=True)
        scales.append(1.0 / jnp.sqrt(value))
    scale = jnp.concatenate(scales, axis=0)
    lane = lax.broadcasted_iota(jnp.int32, (subs, LANES), 1)
    scale = halves(jnp.where(lane < prims, scale, 0.0))
    period = 3 * LANES
    row, col = iotas(LANES, period)
    spread = jnp.where(row == col % prims, 1.0, 0.0).astype(jnp.bfloat16)
    right = sum(jnp.dot(part, spread, preferred_element_type=jnp.float32) for part in scale)
    for block in range(prims * prims // period):
        pick = jnp.where(row == col // prims + block * (period // prims), 1.0, 0.0).astype(jnp.bfloat16)
        left = sum(jnp.dot(part, pick, preferred_element_type=jnp.float32) for part in scale)
        lanes = slice(block * period, (block + 1) * period)
        half = subs // galerkin_ref.shape[0]
        for m in range(galerkin_ref.shape[0]):
            rows = slice(m * half, (m + 1) * half)
            out_ref[rows, lanes] = left[rows] * galerkin_ref[m, :, lanes] * right[rows]


def scale_blocks(indices, table, gathered):
    members, subs, size = gathered.shape
    per_step = 2
    return pl.pallas_call(
        scale_kernel,
        out_shape=jax.ShapeDtypeStruct((members * subs, size), jnp.float32),
        grid=(members // per_step,),
        in_specs=[
            pl.BlockSpec((per_step * subs, LANES), lambda i: (i, 0)),
            pl.BlockSpec(table.shape, lambda i: (0, 0)),
            pl.BlockSpec((per_step, subs, size), lambda i: (i, 0, 0)),
        ],
        out_specs=pl.BlockSpec((per_step * subs, size), lambda i: (i, 0)),
        name="scale_blocks",
    )(indices, table, gathered)


def everywhere(block):
    devices = lax.axis_size("group") * lax.axis_size("member")
    copies = jnp.broadcast_to(block[None], (devices,) + block.shape)
    return lax.all_to_all(copies, AXES, split_axis=0, concat_axis=0, tiled=True)


def local(face_schur, face_inverse, face_basis, partner, prim_index):
    subs, _, prims, width = face_basis.shape
    count = subs * 6
    members = lax.axis_size("member")
    groups = lax.axis_size("group")
    schur = face_schur.reshape(count, width, width)
    inverse = face_inverse.reshape(count, width, width)
    basis = face_basis.reshape(count, prims, width)
    slots = partner.reshape(count) // count % members
    padded_index = jnp.pad(prim_index, ((0, 0), (0, LANES - prims)), constant_values=-1)
    indices = everywhere(padded_index).reshape(groups * members * subs, LANES)
    sent = pack(slots, schur, inverse, members)
    received = lax.all_to_all(sent, "member", split_axis=0, concat_axis=0, tiled=True)
    deluxe, galerkin, diagonal = faces(slots, schur, inverse, basis, received, subs)
    values = everywhere(diagonal[:subs]).reshape(groups * members * subs, LANES)
    flat = galerkin.reshape(subs, prims * prims)
    gathered = lax.all_to_all(
        jnp.broadcast_to(flat[None], (members,) + flat.shape),
        "member", split_axis=0, concat_axis=0, tiled=True,
    )
    table = coarse_table(indices, values, COARSE_PER_SUB * subs * groups * members)
    start = lax.axis_index("group") * members * subs
    own = lax.dynamic_slice_in_dim(indices, start, members * subs, axis=0)
    blocks = scale_blocks(own, table, gathered)
    return deluxe.reshape(face_basis.shape), blocks


def solution(mesh):
    split = P(AXES, None, None, None)
    in_specs = (split, split, split, P(AXES, None), P(AXES, None))
    out_specs = (split, P("group", None))
    return jax.shard_map(local, mesh=mesh, in_specs=in_specs, out_specs=out_specs, check_vma=False)
```

```python
import jax
import jax.numpy as jnp
from jax import lax
from jax.experimental import pallas as pl
from jax.experimental.pallas import tpu as pltpu
from jax.sharding import PartitionSpec as P

AXES = ("group", "member")
COARSE_PER_SUB = 48
LANES = 128
TAIL = 8
INDEX_ROW = 2


def iotas(rows, cols):
    return (
        lax.broadcasted_iota(jnp.int32, (rows, cols), 0),
        lax.broadcasted_iota(jnp.int32, (rows, cols), 1),
    )


def halves(value):
    high = value.astype(jnp.bfloat16)
    return high, (value - high.astype(jnp.float32)).astype(jnp.bfloat16)


def dot(left, right, right_dim=0):
    dims = (((1,), (right_dim,)), ((), ()))
    rows = left[0].shape[0]
    stacked = jnp.concatenate(left, axis=0)
    first = lax.dot_general(stacked, right[0], dims, preferred_element_type=jnp.float32)
    second = lax.dot_general(left[0], right[1], dims, preferred_element_type=jnp.float32)
    return first[:rows] + (first[rows:] + second)


def pack_kernel(slot_ref, tail_ref, schur_ref, inverse_ref, out_ref, schur_buf, inverse_buf, out_buf, schur_sem, inverse_sem, out_sem, tail_sem):
    count, width = schur_buf.shape[:2]
    members = out_ref.shape[0]
    parts = width // LANES
    body = parts * width

    def load(f):
        return (
            pltpu.make_async_copy(schur_ref.at[f], schur_buf.at[f], schur_sem.at[f]),
            pltpu.make_async_copy(inverse_ref.at[f], inverse_buf.at[f], inverse_sem.at[f]),
        )

    def tail(j):
        return pltpu.make_async_copy(tail_ref, out_ref.at[j, pl.ds(body, TAIL), :], tail_sem.at[j])

    def save(f):
        return pltpu.make_async_copy(out_buf.at[f], out_ref.at[slot_ref[f]], out_sem.at[f])

    for f in range(count):
        for copy in load(f):
            copy.start()
    for j in range(members):
        tail(j).start()
    for j in range(members):
        tail(j).wait()
    row, col = iotas(width, width)
    upper, middle = row <= col, row == col

    @pl.loop(0, count)
    def _(f):
        for copy in load(f):
            copy.wait()
        schur, inverse = schur_buf[f], inverse_buf[f]
        packed = jnp.where(upper, schur, inverse)
        diagonal = jnp.sum(jnp.where(middle, inverse, 0.0), axis=0, keepdims=True)
        for part in range(parts):
            lanes = slice(part * LANES, (part + 1) * LANES)
            out_buf[f, part * width : (part + 1) * width, :] = packed[:, lanes]
        out_buf[f, body : body + TAIL, :] = tail_ref[...]
        for part in range(parts):
            lanes = slice(part * LANES, (part + 1) * LANES)
            out_buf[f, body + part : body + part + 1, :] = diagonal[:, lanes]
        save(f).start()

    for f in range(count):
        save(f).wait()


def pack(slots, tail, schur, inverse, members):
    count, width = schur.shape[:2]
    rows = width * width // LANES + TAIL
    return pl.pallas_call(
        pack_kernel,
        out_shape=jax.ShapeDtypeStruct((members, rows, LANES), jnp.float32),
        in_specs=[
            pl.BlockSpec(memory_space=pltpu.SMEM),
            pl.BlockSpec(memory_space=pltpu.VMEM),
            pl.BlockSpec(memory_space=pl.ANY),
            pl.BlockSpec(memory_space=pl.ANY),
        ],
        out_specs=pl.BlockSpec(memory_space=pl.ANY),
        scratch_shapes=[
            pltpu.VMEM((count, width, width), jnp.float32),
            pltpu.VMEM((count, width, width), jnp.float32),
            pltpu.VMEM((count, rows, LANES), jnp.float32),
            pltpu.SemaphoreType.DMA((count,)),
            pltpu.SemaphoreType.DMA((count,)),
            pltpu.SemaphoreType.DMA((count,)),
            pltpu.SemaphoreType.DMA((members,)),
        ],
        name="pack_faces",
    )(slots, tail, schur, inverse)


def fold(block):
    half = block.shape[0] // 2
    row, col = iotas(half, 2 * half)
    swung = jnp.concatenate([block[half:, :half], block[:half, :half]], axis=1)
    return jnp.where((col < half) | (row > col - half), swung, block[half:, :])


def face_kernel(slot_ref, schur_ref, inverse_ref, basis_ref, *rest):
    per_step = schur_ref.shape[0]
    received = rest[:per_step]
    deluxe_ref, payload_ref, galerkin_ref = rest[per_step:]
    width = schur_ref.shape[1]
    prims = basis_ref.shape[1]
    subs = galerkin_ref.shape[0]
    parts = width // LANES
    body = parts * width
    steps_per_sub = 6 // per_step
    step = pl.program_id(0)
    every = range(per_step)
    row, col = iotas(width, width)
    other_schur, summed, initial = [], [], []
    for f in every:
        mixed = jnp.concatenate([received[f][0, p * width : (p + 1) * width, :] for p in range(parts)], axis=1)
        line = jnp.concatenate([received[f][0, body + p : body + p + 1, :] for p in range(parts)], axis=1)
        turned = mixed.T
        other = jnp.where(row <= col, mixed, turned)
        other_inverse = jnp.where(row > col, mixed, jnp.where(row == col, line, turned))
        summed.append(halves(schur_ref[f] + other))
        initial.append(halves(0.25 * (inverse_ref[f] + other_inverse)))
        other_schur.append(halves(other))
    product = [dot(halves(basis_ref[f]), halves(schur_ref[f])) for f in every]
    residual = [halves(jnp.where(row == col, 1.0, 0.0) - dot(summed[f], initial[f])) for f in every]
    start = [dot(halves(product[f]), initial[f]) for f in every]
    deluxe = start
    for _ in range(3):
        deluxe = [start[f] + dot(halves(deluxe[f]), residual[f]) for f in every]
    for f in every:
        deluxe_ref[f] = deluxe[f]
    deluxe = [halves(d) for d in deluxe]
    weighted = [dot(deluxe[f], other_schur[f]) for f in every]
    total = sum(dot(halves(weighted[f]), deluxe[f], right_dim=1) for f in every)
    sub = step // steps_per_sub

    @pl.when(step % steps_per_sub == 0)
    def _():
        galerkin_ref[sub] = total

    @pl.when(step % steps_per_sub != 0)
    def _():
        galerkin_ref[sub] += total

    @pl.when(step == subs * steps_per_sub - 1)
    def _():
        half = prims // 2
        row, col = iotas(prims, prims)
        blocks = [galerkin_ref[s] for s in range(subs)]
        lines = [jnp.sum(jnp.where(row == col, b, 0.0), axis=0, keepdims=True) for b in blocks]
        payload_ref[:half] = jnp.concatenate([fold(b) for b in blocks], axis=1)
        line = jnp.concatenate(lines, axis=1)
        payload_ref[half:] = jnp.broadcast_to(line, (payload_ref.shape[0] - half, line.shape[1]))


def faces(slots, schur, inverse, basis, received, subs):
    count, width = schur.shape[:2]
    prims = basis.shape[1]
    rows = received.shape[1]
    per_step = 2
    block = pl.BlockSpec((per_step, width, width), lambda i, slot: (i, 0, 0))
    thin = pl.BlockSpec((per_step, prims, width), lambda i, slot: (i, 0, 0))
    payload = (prims // 2 + 8, subs * prims)

    def incoming(offset):
        return pl.BlockSpec((1, rows, LANES), lambda i, slot: (slot[i * per_step + offset], 0, 0))

    return pl.pallas_call(
        face_kernel,
        out_shape=(
            jax.ShapeDtypeStruct((count, prims, width), jnp.float32),
            jax.ShapeDtypeStruct(payload, jnp.float32),
        ),
        grid_spec=pltpu.PrefetchScalarGridSpec(
            num_scalar_prefetch=1,
            grid=(count // per_step,),
            in_specs=[block, block, thin] + [incoming(o) for o in range(per_step)],
            out_specs=(thin, pl.BlockSpec(payload, lambda i, slot: (0, 0))),
            scratch_shapes=[pltpu.VMEM((subs, prims, prims), jnp.float32)],
        ),
        name="face_terms",
    )(slots, schur, inverse, basis, *([received] * per_step))


def digits(ref, m, r):
    index = ref[m, INDEX_ROW + r : INDEX_ROW + r + 1, :].astype(jnp.int32)
    high = lax.shift_right_logical(index, 7)
    return high, index - high * LANES


def table_kernel(index_ref, line_ref, table_ref):
    members = index_ref.shape[0]
    highs = table_ref.shape[0]
    chunks = line_ref.shape[2] // LANES
    high_iota = lax.broadcasted_iota(jnp.int32, (highs, LANES), 0)
    low_iota = lax.broadcasted_iota(jnp.int32, (LANES, LANES), 0)
    dims = (((1,), (1,)), ((), ()))
    group = 4
    table_ref[...] = jnp.zeros_like(table_ref)

    @pl.loop(0, members // group)
    def _(g):
        left, right, rest = [], [], []
        for k in range(group):
            m = g * group + k
            for r in range(chunks):
                high, low = digits(index_ref, m, r)
                value = line_ref[m, 0:1, r * LANES : (r + 1) * LANES]
                coarse = value.astype(jnp.bfloat16).astype(jnp.float32)
                hit = low_iota == low
                left.append(jnp.where(high_iota == high, 1.0, 0.0).astype(jnp.bfloat16))
                right.append(jnp.where(hit, coarse, 0.0).astype(jnp.bfloat16))
                rest.append(jnp.where(hit, value - coarse, 0.0).astype(jnp.bfloat16))
        left = jnp.concatenate(left, axis=1)
        right = jnp.concatenate([jnp.concatenate(right, axis=1), jnp.concatenate(rest, axis=1)], axis=0)
        total = lax.dot_general(left, right, dims, preferred_element_type=jnp.float32)
        table_ref[...] += total[:, :LANES] + total[:, LANES:]


def group_table(received, gathered, coarse):
    members, rows = received.shape[:2]
    payload = gathered.shape[1:]
    highs = coarse // LANES
    return pl.pallas_call(
        table_kernel,
        out_shape=jax.ShapeDtypeStruct((highs, LANES), jnp.float32),
        grid=(1,),
        in_specs=[
            pl.BlockSpec((members, TAIL, LANES), lambda i: (0, rows // TAIL - 1, 0)),
            pl.BlockSpec((members, 8, payload[1]), lambda i: (0, payload[0] // 8 - 1, 0)),
        ],
        out_specs=pl.BlockSpec((highs, LANES), lambda i: (0, 0)),
        name="group_table",
    )(received, gathered)


def scale_kernel(index_ref, payload_ref, *rest):
    *table_refs, out_ref, table_buf, block_buf = rest
    members, rows, lanes = payload_ref.shape
    subs = out_ref.shape[0] // members
    half = rows - 8
    prims = 2 * half
    highs = table_refs[0].shape[0]
    chunks = lanes // LANES

    @pl.when(pl.program_id(0) == 0)
    def _():
        table = sum(ref[...] for ref in table_refs).T
        high, low = halves(table)
        table_buf[:LANES] = high
        table_buf[LANES:] = low

    high_iota = lax.broadcasted_iota(jnp.int32, (highs, LANES), 0)
    low_iota = lax.broadcasted_iota(jnp.int32, (LANES, LANES), 0)
    row, col = iotas(half, prims)
    for m in range(members):
        marks, lows = [], []
        for r in range(chunks):
            high, low = digits(index_ref, m, r)
            marks.append(jnp.where(high_iota == high, 1.0, 0.0).astype(jnp.bfloat16))
            lows.append(low)
        found = jnp.dot(table_buf[...], jnp.concatenate(marks, axis=1), preferred_element_type=jnp.float32)
        found = found[:LANES] + found[LANES:]
        scale = []
        for r in range(chunks):
            hit = jnp.where(low_iota == lows[r], found[:, r * LANES : (r + 1) * LANES], 0.0)
            scale.append(1.0 / jnp.sqrt(jnp.sum(hit, axis=0, keepdims=True)))
        scale = jnp.concatenate(scale, axis=1)
        main = payload_ref[m, :half, :]
        line = payload_ref[m, half : half + 1, :]
        both = jnp.concatenate([main, jnp.broadcast_to(scale, (8, lanes))], axis=0)
        turned = both.T
        for s in range(subs):
            mine = slice(s * prims, (s + 1) * prims)
            flat, mirror = main[:, mine], turned[mine]
            line_s, scale_s = line[:, mine], scale[:, mine]
            column = mirror[:, half : half + 1]
            corner, corner_turned = flat[:, half:], mirror[half:, :half]
            top_corner = jnp.concatenate([corner, mirror[:half, :half]], axis=1)
            top_other = jnp.concatenate([corner_turned, mirror[:half, :half]], axis=1)
            top = jnp.where((row > col) | (col >= half), top_corner, jnp.where(row == col, line_s, top_other))
            low_other = jnp.concatenate([flat[:, :half], corner_turned], axis=1)
            low = jnp.where((row < col - half) | (col < half), flat, jnp.where(row == col - half, line_s, low_other))
            at = (m * subs + s) * prims
            block_buf[at : at + half, :prims] = column[:half] * top * scale_s
            block_buf[at + half : at + prims, :prims] = column[half:] * low * scale_s
    count = members * subs
    span = 4
    for a in range(0, prims, span):
        pieces = [block_buf[pl.ds(a + k, count, stride=prims), :][:, :prims] for k in range(span)]
        out_ref[:, a * prims : (a + span) * prims] = jnp.concatenate(pieces, axis=1)


def scale_blocks(received, gathered, tables, subs):
    members, rows = received.shape[:2]
    payload = gathered.shape[1:]
    prims = payload[1] // subs
    highs = tables[0].shape[0]
    per_step = 2
    whole = pl.BlockSpec((highs, LANES), lambda i: (0, 0))
    return pl.pallas_call(
        scale_kernel,
        out_shape=jax.ShapeDtypeStruct((members * subs, prims * prims), jnp.float32),
        grid=(members // per_step,),
        in_specs=[
            pl.BlockSpec((per_step, TAIL, LANES), lambda i: (i, rows // TAIL - 1, 0)),
            pl.BlockSpec((per_step,) + payload, lambda i: (i, 0, 0)),
        ]
        + [whole] * len(tables),
        out_specs=pl.BlockSpec((per_step * subs, prims * prims), lambda i: (i, 0)),
        scratch_shapes=[
            pltpu.VMEM((2 * LANES, highs), jnp.bfloat16),
            pltpu.VMEM((per_step * subs * prims, LANES), jnp.float32),
        ],
        name="scale_blocks",
    )(received, gathered, *tables)


def exchange(blocks):
    return lax.all_to_all(blocks, "member", split_axis=0, concat_axis=0, tiled=True)


def local(face_schur, face_inverse, face_basis, partner, prim_index):
    subs, _, prims, width = face_basis.shape
    count = subs * 6
    members = lax.axis_size("member")
    groups = lax.axis_size("group")
    schur = face_schur.reshape(count, width, width)
    inverse = face_inverse.reshape(count, width, width)
    basis = face_basis.reshape(count, prims, width)
    slots = lax.rem(lax.div(partner.reshape(count), count), members)
    tail = jnp.pad(prim_index.astype(jnp.float32).reshape(-1, LANES), ((INDEX_ROW, 3), (0, 0)))
    received = exchange(pack(slots, tail, schur, inverse, members))
    deluxe, payload = faces(slots, schur, inverse, basis, received, subs)
    gathered = exchange(jnp.broadcast_to(payload[None], (members,) + payload.shape))
    table = group_table(received, gathered, COARSE_PER_SUB * subs * groups * members)
    tables = [table] + [
        lax.ppermute(table, "group", [(i, (i + k) % groups) for i in range(groups)]) for k in range(1, groups)
    ]
    blocks = scale_blocks(received, gathered, tables, subs)
    return deluxe.reshape(face_basis.shape), blocks


def solution(mesh):
    split = P(AXES, None, None, None)
    in_specs = (split, split, split, P(AXES, None), P(AXES, None))
    out_specs = (split, P("group", None))
    return jax.shard_map(local, mesh=mesh, in_specs=in_specs, out_specs=out_specs, check_vma=False)
```

```python
import jax
import jax.numpy as jnp
from jax import lax
from jax.experimental import pallas as pl
from jax.experimental.pallas import tpu as pltpu
from jax.sharding import PartitionSpec as P

AXES = ("group", "member")
COARSE_PER_SUB = 48
LANES = 128
TAIL = 8
INDEX_ROW = 2
MEMBERS = 32
PER_STEP = 6


def iotas(rows, cols):
    return (
        lax.broadcasted_iota(jnp.int32, (rows, cols), 0),
        lax.broadcasted_iota(jnp.int32, (rows, cols), 1),
    )


def halves(value):
    high = value.astype(jnp.bfloat16)
    return high, (value - high.astype(jnp.float32)).astype(jnp.bfloat16)


def dot(left, right, right_dim=0):
    dims = (((1,), (right_dim,)), ((), ()))
    rows = left[0].shape[0]
    stacked = jnp.concatenate(left, axis=0)
    first = lax.dot_general(stacked, right[0], dims, preferred_element_type=jnp.float32)
    second = lax.dot_general(left[0], right[1], dims, preferred_element_type=jnp.float32)
    return first[:rows] + (first[rows:] + second)


def slot_of(partner_ref, f):
    subs, around = partner_ref.shape
    target = partner_ref[f // around, f % around]
    return lax.rem(lax.div(target, subs * around), MEMBERS)


def pack_kernel(partner_ref, index_ref, schur_ref, inverse_ref, out_ref, tail_ref, schur_buf, inverse_buf, out_buf, schur_sem, inverse_sem, out_sem, tail_sem):
    count, width = schur_buf.shape[:2]
    members = out_ref.shape[0]
    parts = width // LANES
    body = parts * width

    def load(f):
        return (
            pltpu.make_async_copy(schur_ref.at[f], schur_buf.at[f], schur_sem.at[f]),
            pltpu.make_async_copy(inverse_ref.at[f], inverse_buf.at[f], inverse_sem.at[f]),
        )

    def tail(j):
        return pltpu.make_async_copy(tail_ref, out_ref.at[j, pl.ds(body, TAIL), :], tail_sem.at[j])

    def save(f):
        return pltpu.make_async_copy(out_buf.at[f], out_ref.at[slot_of(partner_ref, f)], out_sem.at[f])

    for f in range(count):
        for copy in load(f):
            copy.start()
    index = index_ref[...].astype(jnp.float32)
    tail_ref[...] = jnp.zeros_like(tail_ref)
    rows = deal([index[k : k + 1] for k in range(index.shape[0])])
    for r in range(len(rows)):
        tail_ref[INDEX_ROW + r : INDEX_ROW + r + 1, :] = rows[r]
    for j in range(members):
        tail(j).start()
    for j in range(members):
        tail(j).wait()
    row, col = iotas(width, width)
    upper, middle = row <= col, row == col

    @pl.loop(0, count)
    def _(f):
        for copy in load(f):
            copy.wait()
        schur, inverse = schur_buf[f], inverse_buf[f]
        packed = jnp.where(upper, schur, inverse)
        diagonal = jnp.sum(jnp.where(middle, inverse, 0.0), axis=0, keepdims=True)
        for part in range(parts):
            lanes = slice(part * LANES, (part + 1) * LANES)
            out_buf[f, part * width : (part + 1) * width, :] = packed[:, lanes]
        out_buf[f, body : body + TAIL, :] = tail_ref[...]
        for part in range(parts):
            lanes = slice(part * LANES, (part + 1) * LANES)
            out_buf[f, body + part : body + part + 1, :] = diagonal[:, lanes]
        save(f).start()

    for f in range(count):
        save(f).wait()


def pack(partner, prim_index, schur, inverse, members):
    count, width = schur.shape[:2]
    rows = width * width // LANES + TAIL
    return pl.pallas_call(
        pack_kernel,
        out_shape=jax.ShapeDtypeStruct((members, rows, LANES), jnp.float32),
        in_specs=[
            pl.BlockSpec(memory_space=pltpu.SMEM),
            pl.BlockSpec(memory_space=pltpu.VMEM),
            pl.BlockSpec(memory_space=pl.ANY),
            pl.BlockSpec(memory_space=pl.ANY),
        ],
        out_specs=pl.BlockSpec(memory_space=pl.ANY),
        scratch_shapes=[
            pltpu.VMEM((TAIL, LANES), jnp.float32),
            pltpu.VMEM((count, width, width), jnp.float32),
            pltpu.VMEM((count, width, width), jnp.float32),
            pltpu.VMEM((count, rows, LANES), jnp.float32),
            pltpu.SemaphoreType.DMA((count,)),
            pltpu.SemaphoreType.DMA((count,)),
            pltpu.SemaphoreType.DMA((count,)),
            pltpu.SemaphoreType.DMA((members,)),
        ],
        name="pack_faces",
    )(partner, prim_index, schur, inverse)


def fold(block):
    half = block.shape[0] // 2
    row, col = iotas(half, half)
    corner = jnp.where(row > col, block[:half, :half], block[half:, half:])
    return jnp.concatenate([corner, block[:half, half:]], axis=1)


def deal(pieces):
    extra = LANES - pieces[0].shape[1]
    return [
        jnp.concatenate([pieces[r], pieces[3][:, r * extra : (r + 1) * extra]], axis=1) for r in range(3)
    ]


def face_kernel(partner_ref, schur_ref, inverse_ref, basis_ref, *rest):
    per_step = schur_ref.shape[0]
    received = rest[:per_step]
    deluxe_ref, payload_ref, galerkin_ref = rest[per_step:]
    width = schur_ref.shape[1]
    prims = basis_ref.shape[1]
    subs = galerkin_ref.shape[0]
    parts = width // LANES
    body = parts * width
    steps_per_sub = 6 // per_step
    step = pl.program_id(0)
    every = range(per_step)
    row, col = iotas(width, width)
    other_schur, summed, initial = [], [], []
    for f in every:
        mixed = jnp.concatenate([received[f][0, p * width : (p + 1) * width, :] for p in range(parts)], axis=1)
        line = jnp.concatenate([received[f][0, body + p : body + p + 1, :] for p in range(parts)], axis=1)
        turned = mixed.T
        other = jnp.where(row <= col, mixed, turned)
        other_inverse = jnp.where(row > col, mixed, jnp.where(row == col, line, turned))
        summed.append(schur_ref[f] + other)
        initial.append(halves(0.25 * (inverse_ref[f] + other_inverse)))
        other_schur.append(halves(other))
    product = [dot(halves(basis_ref[f]), halves(schur_ref[f])) for f in every]
    both = [halves(jnp.concatenate([summed[f], product[f]], axis=0)) for f in every]
    both = [dot(both[f], initial[f]) for f in every]
    residual = [halves(jnp.where(row == col, 1.0, 0.0) - both[f][:width]) for f in every]
    start = [both[f][width:] for f in every]
    deluxe = start
    for _ in range(3):
        deluxe = [start[f] + dot(halves(deluxe[f]), residual[f]) for f in every]
    for f in every:
        deluxe_ref[f] = deluxe[f]
    deluxe = [halves(d) for d in deluxe]
    weighted = [dot(deluxe[f], other_schur[f]) for f in every]
    total = sum(dot(halves(weighted[f]), deluxe[f], right_dim=1) for f in every)
    sub = step // steps_per_sub

    @pl.when(step % steps_per_sub == 0)
    def _():
        galerkin_ref[sub] = total

    @pl.when(step % steps_per_sub != 0)
    def _():
        galerkin_ref[sub] += total

    @pl.when(step == subs * steps_per_sub - 1)
    def _():
        half = prims // 2
        row, col = iotas(prims, prims)
        blocks = [galerkin_ref[s] for s in range(subs)]
        lines = [jnp.sum(jnp.where(row == col, b, 0.0), axis=0, keepdims=True) for b in blocks]
        payload_ref[:half] = jnp.concatenate(deal([fold(b) for b in blocks]), axis=1)
        line = jnp.concatenate(deal(lines), axis=1)
        payload_ref[half:] = jnp.broadcast_to(line, (payload_ref.shape[0] - half, line.shape[1]))


def faces(partner, schur, inverse, basis, received, subs):
    count, width = schur.shape[:2]
    prims = basis.shape[1]
    rows = received.shape[1]
    per_step = PER_STEP
    block = pl.BlockSpec((per_step, width, width), lambda i, partner: (i, 0, 0))
    thin = pl.BlockSpec((per_step, prims, width), lambda i, partner: (i, 0, 0))
    payload = (prims // 2 + 8, subs * prims)

    def incoming(offset):
        return pl.BlockSpec((1, rows, LANES), lambda i, partner: (slot_of(partner, i * per_step + offset), 0, 0))

    return pl.pallas_call(
        face_kernel,
        out_shape=(
            jax.ShapeDtypeStruct((count, prims, width), jnp.float32),
            jax.ShapeDtypeStruct(payload, jnp.float32),
        ),
        grid_spec=pltpu.PrefetchScalarGridSpec(
            num_scalar_prefetch=1,
            grid=(count // per_step,),
            in_specs=[block, block, thin] + [incoming(o) for o in range(per_step)],
            out_specs=(thin, pl.BlockSpec(payload, lambda i, partner: (0, 0))),
            scratch_shapes=[pltpu.VMEM((subs, prims, prims), jnp.float32)],
        ),
        name="face_terms",
    )(partner, schur, inverse, basis, *([received] * per_step))


def digits(ref, m, r):
    index = ref[m, INDEX_ROW + r : INDEX_ROW + r + 1, :].astype(jnp.int32)
    high = lax.shift_right_logical(index, 7)
    return high, index - high * LANES


def table_kernel(index_ref, line_ref, table_ref):
    members = index_ref.shape[0]
    highs = table_ref.shape[0]
    chunks = line_ref.shape[2] // LANES
    high_iota = lax.broadcasted_iota(jnp.int32, (highs, LANES), 0)
    low_iota = lax.broadcasted_iota(jnp.int32, (LANES, LANES), 0)
    dims = (((1,), (1,)), ((), ()))
    group = 4
    table_ref[...] = jnp.zeros_like(table_ref)

    @pl.loop(0, members // group)
    def _(g):
        left, right, rest = [], [], []
        for k in range(group):
            m = g * group + k
            for r in range(chunks):
                high, low = digits(index_ref, m, r)
                value = line_ref[m, 0:1, r * LANES : (r + 1) * LANES]
                coarse = value.astype(jnp.bfloat16).astype(jnp.float32)
                hit = low_iota == low
                left.append(jnp.where(high_iota == high, 1.0, 0.0).astype(jnp.bfloat16))
                right.append(jnp.where(hit, coarse, 0.0).astype(jnp.bfloat16))
                rest.append(jnp.where(hit, value - coarse, 0.0).astype(jnp.bfloat16))
        left = jnp.concatenate(left, axis=1)
        right = jnp.concatenate([jnp.concatenate(right, axis=1), jnp.concatenate(rest, axis=1)], axis=0)
        total = lax.dot_general(left, right, dims, preferred_element_type=jnp.float32)
        table_ref[...] += total[:, :LANES] + total[:, LANES:]


def group_table(received, gathered, coarse):
    members, rows = received.shape[:2]
    payload = gathered.shape[1:]
    highs = coarse // LANES
    return pl.pallas_call(
        table_kernel,
        out_shape=jax.ShapeDtypeStruct((highs, LANES), jnp.float32),
        grid=(1,),
        in_specs=[
            pl.BlockSpec((members, TAIL, LANES), lambda i: (0, rows // TAIL - 1, 0)),
            pl.BlockSpec((members, 8, payload[1]), lambda i: (0, payload[0] // 8 - 1, 0)),
        ],
        out_specs=pl.BlockSpec((highs, LANES), lambda i: (0, 0)),
        name="group_table",
    )(received, gathered)


def scale_kernel(index_ref, payload_ref, *rest):
    *table_refs, out_ref, table_buf, block_buf = rest
    members, rows, lanes = payload_ref.shape
    subs = out_ref.shape[0] // members
    half = rows - 8
    prims = 2 * half
    highs = table_refs[0].shape[0]
    chunks = lanes // LANES

    @pl.when(pl.program_id(0) == 0)
    def _():
        table = sum(ref[...] for ref in table_refs).T
        high, low = halves(table)
        table_buf[:LANES] = high
        table_buf[LANES:] = low

    high_iota = lax.broadcasted_iota(jnp.int32, (highs, LANES), 0)
    low_iota = lax.broadcasted_iota(jnp.int32, (LANES, LANES), 0)
    row, col = iotas(half, LANES)
    for m in range(members):
        marks, lows = [], []
        for r in range(chunks):
            high, low = digits(index_ref, m, r)
            marks.append(jnp.where(high_iota == high, 1.0, 0.0).astype(jnp.bfloat16))
            lows.append(low)
        found = jnp.dot(table_buf[...], jnp.concatenate(marks, axis=1), preferred_element_type=jnp.float32)
        found = found[:LANES] + found[LANES:]
        scale = []
        for r in range(chunks):
            hit = jnp.where(low_iota == lows[r], found[:, r * LANES : (r + 1) * LANES], 0.0)
            scale.append(1.0 / jnp.sqrt(jnp.sum(hit, axis=0, keepdims=True)))
        main, lines, turned = [], [], []
        for r in range(chunks):
            across = slice(r * LANES, (r + 1) * LANES)
            main.append(payload_ref[m, :half, across])
            lines.append(payload_ref[m, half : half + 1, across])
            turned.append(jnp.concatenate([main[r], jnp.broadcast_to(scale[r], (8, LANES))], axis=0).T)

        def gather(parts, axis):
            parts = [lax.slice_in_dim(p, prims, LANES, axis=axis) for p in parts]
            return jnp.concatenate(parts + [parts[0]], axis=axis)

        for s in range(subs):
            last = s == subs - 1
            flat = gather(main, 1) if last else main[s]
            line = gather(lines, 1) if last else lines[s]
            scale_s = gather(scale, 1) if last else scale[s]
            mirror = gather(turned, 0) if last else turned[s]
            column = mirror[:prims, half : half + 1]
            mirror = jnp.concatenate([mirror[:prims], jnp.zeros((prims, LANES - mirror.shape[1]), jnp.float32)], axis=1)
            top = jnp.where((col >= half) | (row > col), flat, jnp.where(row == col, line, mirror[:half]))
            shifted = jnp.concatenate([line[:, half:], line[:, :half]], axis=1)
            corner = jnp.where(row < col, flat, jnp.where(row == col, shifted, mirror[:half]))
            low = jnp.concatenate([mirror[half:, :half], corner[:, : LANES - half]], axis=1)
            at = (m * subs + s) * prims
            block_buf[at : at + half] = column[:half] * top * scale_s
            block_buf[at + half : at + prims] = column[half:] * low * scale_s
    count = members * subs
    span = 4
    for a in range(0, prims, span):
        pieces = [block_buf[pl.ds(a + k, count, stride=prims), :][:, :prims] for k in range(span)]
        out_ref[:, a * prims : (a + span) * prims] = jnp.concatenate(pieces, axis=1)


def scale_blocks(received, gathered, tables, subs):
    members, rows = received.shape[:2]
    payload = gathered.shape[1:]
    prims = payload[1] // subs
    highs = tables[0].shape[0]
    per_step = 2
    whole = pl.BlockSpec((highs, LANES), lambda i: (0, 0))
    return pl.pallas_call(
        scale_kernel,
        out_shape=jax.ShapeDtypeStruct((members * subs, prims * prims), jnp.float32),
        grid=(members // per_step,),
        in_specs=[
            pl.BlockSpec((per_step, TAIL, LANES), lambda i: (i, rows // TAIL - 1, 0)),
            pl.BlockSpec((per_step,) + payload, lambda i: (i, 0, 0)),
        ]
        + [whole] * len(tables),
        out_specs=pl.BlockSpec((per_step * subs, prims * prims), lambda i: (i, 0)),
        scratch_shapes=[
            pltpu.VMEM((2 * LANES, highs), jnp.bfloat16),
            pltpu.VMEM((per_step * subs * prims, LANES), jnp.float32),
        ],
        name="scale_blocks",
    )(received, gathered, *tables)


def exchange(blocks):
    return lax.all_to_all(blocks, "member", split_axis=0, concat_axis=0, tiled=True)


def local(face_schur, face_inverse, face_basis, partner, prim_index):
    subs, _, prims, width = face_basis.shape
    count = subs * 6
    members = lax.axis_size("member")
    groups = lax.axis_size("group")
    schur = face_schur.reshape(count, width, width)
    inverse = face_inverse.reshape(count, width, width)
    basis = face_basis.reshape(count, prims, width)
    received = exchange(pack(partner, prim_index, schur, inverse, members))
    deluxe, payload = faces(partner, schur, inverse, basis, received, subs)
    gathered = exchange(jnp.broadcast_to(payload[None], (members,) + payload.shape))
    table = group_table(received, gathered, COARSE_PER_SUB * subs * groups * members)
    tables = [table] + [
        lax.ppermute(table, "group", [(i, (i + k) % groups) for i in range(groups)]) for k in range(1, groups)
    ]
    blocks = scale_blocks(received, gathered, tables, subs)
    return deluxe.reshape(face_basis.shape), blocks


def solution(mesh):
    split = P(AXES, None, None, None)
    in_specs = (split, split, split, P(AXES, None), P(AXES, None))
    out_specs = (split, P("group", None))
    return jax.shard_map(local, mesh=mesh, in_specs=in_specs, out_specs=out_specs, check_vma=False)
```

```python
import jax
import jax.numpy as jnp
from jax import lax
from jax.experimental import pallas as pl
from jax.experimental.pallas import tpu as pltpu
from jax.sharding import PartitionSpec as P

AXES = ("group", "member")
COARSE_PER_SUB = 48
LANES = 128
TAIL = 8
INDEX_ROW = 2
CHUNKS = 3
MEMBERS = 32
PER_STEP = 6


def iotas(rows, cols):
    return (
        lax.broadcasted_iota(jnp.int32, (rows, cols), 0),
        lax.broadcasted_iota(jnp.int32, (rows, cols), 1),
    )


def halves(value):
    high = value.astype(jnp.bfloat16)
    return high, (value - high.astype(jnp.float32)).astype(jnp.bfloat16)


def dot(left, right, right_dim=0):
    dims = (((1,), (right_dim,)), ((), ()))
    rows = left[0].shape[0]
    stacked = jnp.concatenate(left, axis=0)
    first = lax.dot_general(stacked, right[0], dims, preferred_element_type=jnp.float32)
    second = lax.dot_general(left[0], right[1], dims, preferred_element_type=jnp.float32)
    return first[:rows] + (first[rows:] + second)


def slot_of(partner_ref, f):
    subs, around = partner_ref.shape
    target = partner_ref[f // around, f % around]
    return lax.rem(lax.div(target, subs * around), MEMBERS)


def pack_kernel(partner_ref, index_ref, schur_ref, inverse_ref, out_ref, tail_ref, schur_buf, inverse_buf, out_buf, schur_sem, inverse_sem, out_sem, tail_sem):
    count, width = schur_buf.shape[:2]
    members = out_ref.shape[0]
    parts = width // LANES
    body = parts * width

    upper_half, lower_half = pl.ds(0, LANES), pl.ds(width - LANES, LANES)
    pieces = (
        (schur_ref, schur_buf, schur_sem, ((upper_half, slice(None)), (lower_half, lower_half))),
        (inverse_ref, inverse_buf, inverse_sem, ((lower_half, slice(None)), (upper_half, upper_half))),
    )

    def load(f):
        return [
            pltpu.make_async_copy(src.at[f, *part], dst.at[f, *part], sem.at[k, f])
            for src, dst, sem, parts in pieces
            for k, part in enumerate(parts)
        ]

    def tail(j):
        return pltpu.make_async_copy(tail_ref, out_ref.at[j, pl.ds(body, TAIL), :], tail_sem.at[j])

    def save(f):
        return pltpu.make_async_copy(out_buf.at[f], out_ref.at[slot_of(partner_ref, f)], out_sem.at[f])

    for f in range(count):
        for copy in load(f):
            copy.start()
    index = index_ref[...].astype(jnp.float32)
    tail_ref[...] = jnp.zeros_like(tail_ref)
    rows = deal([index[k : k + 1] for k in range(index.shape[0])])
    for r in range(len(rows)):
        tail_ref[INDEX_ROW + r : INDEX_ROW + r + 1, :] = rows[r]
    for j in range(members):
        tail(j).start()
    for j in range(members):
        tail(j).wait()
    row, col = iotas(width, width)
    upper, middle = row <= col, row == col

    @pl.loop(0, count)
    def _(f):
        for copy in load(f):
            copy.wait()
        schur, inverse = schur_buf[f], inverse_buf[f]
        packed = jnp.where(upper, schur, inverse)
        diagonal = jnp.sum(jnp.where(middle, inverse, 0.0), axis=0, keepdims=True)
        for part in range(parts):
            lanes = slice(part * LANES, (part + 1) * LANES)
            out_buf[f, part * width : (part + 1) * width, :] = packed[:, lanes]
        out_buf[f, body : body + TAIL, :] = tail_ref[...]
        for part in range(parts):
            lanes = slice(part * LANES, (part + 1) * LANES)
            out_buf[f, body + part : body + part + 1, :] = diagonal[:, lanes]
        save(f).start()

    for f in range(count):
        save(f).wait()


def pack(partner, prim_index, schur, inverse, members):
    count, width = schur.shape[:2]
    rows = width * width // LANES + TAIL
    return pl.pallas_call(
        pack_kernel,
        out_shape=jax.ShapeDtypeStruct((members, rows, LANES), jnp.float32),
        in_specs=[
            pl.BlockSpec(memory_space=pltpu.SMEM),
            pl.BlockSpec(memory_space=pltpu.VMEM),
            pl.BlockSpec(memory_space=pl.ANY),
            pl.BlockSpec(memory_space=pl.ANY),
        ],
        out_specs=pl.BlockSpec(memory_space=pl.ANY),
        scratch_shapes=[
            pltpu.VMEM((TAIL, LANES), jnp.float32),
            pltpu.VMEM((count, width, width), jnp.float32),
            pltpu.VMEM((count, width, width), jnp.float32),
            pltpu.VMEM((count, rows, LANES), jnp.float32),
            pltpu.SemaphoreType.DMA((2, count)),
            pltpu.SemaphoreType.DMA((2, count)),
            pltpu.SemaphoreType.DMA((count,)),
            pltpu.SemaphoreType.DMA((members,)),
        ],
        name="pack_faces",
    )(partner, prim_index, schur, inverse)


def fold(block):
    half = block.shape[0] // 2
    row, col = iotas(half, half)
    corner = jnp.where(row > col, block[:half, :half], block[half:, half:])
    return jnp.concatenate([corner, block[:half, half:]], axis=1)


def deal(pieces):
    extra = LANES - pieces[0].shape[1]
    return [
        jnp.concatenate([pieces[r], pieces[3][:, r * extra : (r + 1) * extra]], axis=1) for r in range(3)
    ]


def face_kernel(partner_ref, schur_ref, inverse_ref, basis_ref, *rest):
    per_step = schur_ref.shape[0]
    received = rest[:per_step]
    deluxe_ref, payload_ref, galerkin_ref = rest[per_step:]
    width = schur_ref.shape[1]
    prims = basis_ref.shape[1]
    subs = galerkin_ref.shape[0]
    parts = width // LANES
    body = parts * width
    steps_per_sub = 6 // per_step
    step = pl.program_id(0)
    every = range(per_step)
    row, col = iotas(width, width)
    other_schur, summed, initial = [], [], []
    for f in every:
        mixed = jnp.concatenate([received[f][0, p * width : (p + 1) * width, :] for p in range(parts)], axis=1)
        line = jnp.concatenate([received[f][0, body + p : body + p + 1, :] for p in range(parts)], axis=1)
        turned = mixed.T
        other = jnp.where(row <= col, mixed, turned)
        other_inverse = jnp.where(row > col, mixed, jnp.where(row == col, line, turned))
        summed.append(schur_ref[f] + other)
        initial.append(halves(0.25 * (inverse_ref[f] + other_inverse)))
        other_schur.append(halves(other))
    product = [dot(halves(basis_ref[f]), halves(schur_ref[f])) for f in every]
    both = [halves(jnp.concatenate([summed[f], product[f]], axis=0)) for f in every]
    both = [dot(both[f], initial[f]) for f in every]
    residual = [halves(jnp.where(row == col, 1.0, 0.0) - both[f][:width]) for f in every]
    start = [both[f][width:] for f in every]
    deluxe = start
    for _ in range(3):
        deluxe = [start[f] + dot(halves(deluxe[f]), residual[f]) for f in every]
    for f in every:
        deluxe_ref[f] = deluxe[f]
    deluxe = [halves(d) for d in deluxe]
    weighted = [dot(deluxe[f], other_schur[f]) for f in every]
    total = sum(dot(halves(weighted[f]), deluxe[f], right_dim=1) for f in every)
    sub = step // steps_per_sub

    @pl.when(step % steps_per_sub == 0)
    def _():
        galerkin_ref[sub] = total

    @pl.when(step % steps_per_sub != 0)
    def _():
        galerkin_ref[sub] += total

    @pl.when(step == subs * steps_per_sub - 1)
    def _():
        half = prims // 2
        row, col = iotas(prims, prims)
        blocks = [galerkin_ref[s] for s in range(subs)]
        lines = [jnp.sum(jnp.where(row == col, b, 0.0), axis=0, keepdims=True) for b in blocks]
        pieces, lines = deal([fold(b) for b in blocks]), deal(lines)
        payload_ref[...] = jnp.concatenate(pieces + lines + [lines[0]] * (TAIL - len(lines)), axis=0)


def faces(partner, schur, inverse, basis, received, subs):
    count, width = schur.shape[:2]
    prims = basis.shape[1]
    rows = received.shape[1]
    per_step = PER_STEP
    block = pl.BlockSpec((per_step, width, width), lambda i, partner: (i, 0, 0))
    thin = pl.BlockSpec((per_step, prims, width), lambda i, partner: (i, 0, 0))
    payload = (subs * prims * prims // 2 // LANES + TAIL, LANES)

    def incoming(offset):
        return pl.BlockSpec((1, rows, LANES), lambda i, partner: (slot_of(partner, i * per_step + offset), 0, 0))

    return pl.pallas_call(
        face_kernel,
        out_shape=(
            jax.ShapeDtypeStruct((count, prims, width), jnp.float32),
            jax.ShapeDtypeStruct(payload, jnp.float32),
        ),
        grid_spec=pltpu.PrefetchScalarGridSpec(
            num_scalar_prefetch=1,
            grid=(count // per_step,),
            in_specs=[block, block, thin] + [incoming(o) for o in range(per_step)],
            out_specs=(thin, pl.BlockSpec(payload, lambda i, partner: (0, 0))),
            scratch_shapes=[pltpu.VMEM((subs, prims, prims), jnp.float32)],
        ),
        name="face_terms",
    )(partner, schur, inverse, basis, *([received] * per_step))


def digits(ref, m, r):
    index = ref[m, INDEX_ROW + r : INDEX_ROW + r + 1, :].astype(jnp.int32)
    high = lax.shift_right_logical(index, 7)
    return high, index - high * LANES


def table_kernel(index_ref, line_ref, table_ref):
    members = index_ref.shape[0]
    highs = table_ref.shape[0]
    chunks = CHUNKS
    high_iota = lax.broadcasted_iota(jnp.int32, (highs, LANES), 0)
    low_iota = lax.broadcasted_iota(jnp.int32, (LANES, LANES), 0)
    dims = (((1,), (1,)), ((), ()))
    group = 4
    table_ref[...] = jnp.zeros_like(table_ref)

    @pl.loop(0, members // group)
    def _(g):
        left, right, rest = [], [], []
        for k in range(group):
            m = g * group + k
            for r in range(chunks):
                high, low = digits(index_ref, m, r)
                value = line_ref[m, r : r + 1, :]
                coarse = value.astype(jnp.bfloat16).astype(jnp.float32)
                hit = low_iota == low
                left.append(jnp.where(high_iota == high, 1.0, 0.0).astype(jnp.bfloat16))
                right.append(jnp.where(hit, coarse, 0.0).astype(jnp.bfloat16))
                rest.append(jnp.where(hit, value - coarse, 0.0).astype(jnp.bfloat16))
        left = jnp.concatenate(left, axis=1)
        right = jnp.concatenate([jnp.concatenate(right, axis=1), jnp.concatenate(rest, axis=1)], axis=0)
        total = lax.dot_general(left, right, dims, preferred_element_type=jnp.float32)
        table_ref[...] += total[:, :LANES] + total[:, LANES:]


def group_table(received, gathered, coarse):
    members, rows = received.shape[:2]
    payload = gathered.shape[1:]
    highs = coarse // LANES
    return pl.pallas_call(
        table_kernel,
        out_shape=jax.ShapeDtypeStruct((highs, LANES), jnp.float32),
        grid=(1,),
        in_specs=[
            pl.BlockSpec((members, TAIL, LANES), lambda i: (0, rows // TAIL - 1, 0)),
            pl.BlockSpec((members, TAIL, LANES), lambda i: (0, payload[0] // TAIL - 1, 0)),
        ],
        out_specs=pl.BlockSpec((highs, LANES), lambda i: (0, 0)),
        name="group_table",
    )(received, gathered)


def scale_kernel(index_ref, payload_ref, *rest):
    *table_refs, out_ref, table_buf, block_buf = rest
    members, rows, lanes = payload_ref.shape
    subs = out_ref.shape[0] // members
    half = (rows - TAIL) // CHUNKS
    prims = 2 * half
    highs = table_refs[0].shape[0]
    chunks = CHUNKS

    @pl.when(pl.program_id(0) == 0)
    def _():
        table = sum(ref[...] for ref in table_refs).T
        high, low = halves(table)
        table_buf[:LANES] = high
        table_buf[LANES:] = low

    high_iota = lax.broadcasted_iota(jnp.int32, (highs, LANES), 0)
    low_iota = lax.broadcasted_iota(jnp.int32, (LANES, LANES), 0)
    row, col = iotas(half, LANES)
    for m in range(members):
        marks, lows = [], []
        for r in range(chunks):
            high, low = digits(index_ref, m, r)
            marks.append(jnp.where(high_iota == high, 1.0, 0.0).astype(jnp.bfloat16))
            lows.append(low)
        found = jnp.dot(table_buf[...], jnp.concatenate(marks, axis=1), preferred_element_type=jnp.float32)
        found = found[:LANES] + found[LANES:]
        scale = []
        for r in range(chunks):
            hit = jnp.where(low_iota == lows[r], found[:, r * LANES : (r + 1) * LANES], 0.0)
            scale.append(1.0 / jnp.sqrt(jnp.sum(hit, axis=0, keepdims=True)))
        main, lines, turned = [], [], []
        for r in range(chunks):
            main.append(payload_ref[m, r * half : (r + 1) * half, :])
            lines.append(payload_ref[m, chunks * half + r : chunks * half + r + 1, :])
            turned.append(jnp.concatenate([main[r], jnp.broadcast_to(scale[r], (8, LANES))], axis=0).T)

        def gather(parts, axis):
            parts = [lax.slice_in_dim(p, prims, LANES, axis=axis) for p in parts]
            return jnp.concatenate(parts + [parts[0]], axis=axis)

        for s in range(subs):
            last = s == subs - 1
            flat = gather(main, 1) if last else main[s]
            line = gather(lines, 1) if last else lines[s]
            scale_s = gather(scale, 1) if last else scale[s]
            mirror = gather(turned, 0) if last else turned[s]
            column = mirror[:prims, half : half + 1]
            mirror = jnp.concatenate([mirror[:prims], jnp.zeros((prims, LANES - mirror.shape[1]), jnp.float32)], axis=1)
            top = jnp.where((col >= half) | (row > col), flat, jnp.where(row == col, line, mirror[:half]))
            shifted = jnp.concatenate([line[:, half:], line[:, :half]], axis=1)
            corner = jnp.where(row < col, flat, jnp.where(row == col, shifted, mirror[:half]))
            low = jnp.concatenate([mirror[half:, :half], corner[:, : LANES - half]], axis=1)
            at = (m * subs + s) * prims
            block_buf[at : at + half] = column[:half] * top * scale_s
            block_buf[at + half : at + prims] = column[half:] * low * scale_s
    count = members * subs
    span = 4
    for a in range(0, prims, span):
        pieces = [block_buf[pl.ds(a + k, count, stride=prims), :][:, :prims] for k in range(span)]
        out_ref[:, a * prims : (a + span) * prims] = jnp.concatenate(pieces, axis=1)


def scale_blocks(received, gathered, tables, subs):
    members, rows = received.shape[:2]
    payload = gathered.shape[1:]
    prims = 2 * (payload[0] - TAIL) // CHUNKS
    highs = tables[0].shape[0]
    per_step = 2
    whole = pl.BlockSpec((highs, LANES), lambda i: (0, 0))
    return pl.pallas_call(
        scale_kernel,
        out_shape=jax.ShapeDtypeStruct((members * subs, prims * prims), jnp.float32),
        grid=(members // per_step,),
        in_specs=[
            pl.BlockSpec((per_step, TAIL, LANES), lambda i: (i, rows // TAIL - 1, 0)),
            pl.BlockSpec((per_step,) + payload, lambda i: (i, 0, 0)),
        ]
        + [whole] * len(tables),
        out_specs=pl.BlockSpec((per_step * subs, prims * prims), lambda i: (i, 0)),
        scratch_shapes=[
            pltpu.VMEM((2 * LANES, highs), jnp.bfloat16),
            pltpu.VMEM((per_step * subs * prims, LANES), jnp.float32),
        ],
        name="scale_blocks",
    )(received, gathered, *tables)


def exchange(blocks):
    return lax.all_to_all(blocks, "member", split_axis=0, concat_axis=0, tiled=True)


def local(face_schur, face_inverse, face_basis, partner, prim_index):
    subs, _, prims, width = face_basis.shape
    count = subs * 6
    members = lax.axis_size("member")
    groups = lax.axis_size("group")
    schur = face_schur.reshape(count, width, width)
    inverse = face_inverse.reshape(count, width, width)
    basis = face_basis.reshape(count, prims, width)
    received = exchange(pack(partner, prim_index, schur, inverse, members))
    deluxe, payload = faces(partner, schur, inverse, basis, received, subs)
    gathered = exchange(jnp.broadcast_to(payload[None], (members,) + payload.shape))
    table = group_table(received, gathered, COARSE_PER_SUB * subs * groups * members)
    tables = [table] + [
        lax.ppermute(table, "group", [(i, (i + k) % groups) for i in range(groups)]) for k in range(1, groups)
    ]
    blocks = scale_blocks(received, gathered, tables, subs)
    return deluxe.reshape(face_basis.shape), blocks


def solution(mesh):
    split = P(AXES, None, None, None)
    in_specs = (split, split, split, P(AXES, None), P(AXES, None))
    out_specs = (split, P("group", None))
    return jax.shard_map(local, mesh=mesh, in_specs=in_specs, out_specs=out_specs, check_vma=False)
```
